32 devices in a mesh: group: 2 (over x), row: 8 (over z, y), expert: 2 (over core).
Axes of the slice: x: 2, y: 2, z: 4, core: 2. Of those that a mesh axis runs over, the one named last changes fastest.
Arguments:
- tokens: bfloat16 [2, 128, 128, 1024], P('group', ('row', 'expert')), parts along dimension 0, may hold values from -30 to 30
- ln_first: float32 [1024], replicated, may hold values from 0.5 to 1.5
- spec_first: bfloat16 [2, 8, 128, 128], replicated, may hold values from -0.375 to 0.375
- spec_second: bfloat16 [2, 8, 128, 128], replicated, may hold values from -0.375 to 0.375
- spec_bias: float32 [2, 1024], replicated, may hold values from -3 to 3
- ln_second: float32 [1024], replicated, may hold values from 0.5 to 1.5
- routing: int32 [2, 128, 128, 4], P('group', ('row', 'expert')), parts along dimension 0, may hold values from 0 to 3, as said below
- combine: float32 [2, 128, 128, 4], P('group', ('row', 'expert')), parts along dimension 0, may hold values from 0.1 to 0.6
- up_weight: bfloat16 [8, 1024, 1536], P('row'), may hold values from -0.1875 to 0.1875
- down_weight: bfloat16 [8, 1536, 1024], P('row'), may hold values from -0.109375 to 0.109375
Outputs:
- block_out: bfloat16 [2, 128, 128, 1024], P('group', ('row', 'expert')), parts along dimension 0
The draws below stay inside these ranges and needn't reach their ends.
There are 2 independent parts, one for each index of `group`. The reference program is written for one: setup_inputs(seed, part) draws one part's arguments, and reference() takes and returns one part's arrays. A program takes and returns all parts, laid end to end along the dimension named above; an argument that names none is the same for every part. Nothing has to cross between parts.
Inputs may be any that keep to these rules, and one draw needn't show every extreme that they name: `routing`: each token names 4 different experts, and the 1024 tokens held by each index of row+expert name every expert exactly 1024 times.
All inputs are finite; a program needn't handle non-finite values.
Results may differ from the reference program's by a relative error of at most 0.006.
Values may be sent and summed in bfloat16 or wider, within the bound.
A program may use at most 128 MiB of HBM per device.

```python
import math
import jax
import jax.numpy as jnp
from jax import lax

GRID = 128
D = 1024
FF = 3072
NB = 8
TOPK = 4
GRIDS = 1
TOK_DEV = 1024
EXPERTS = 4


def draw_tokens(key, part):
    key_base, key_row, key_col = jax.random.split(jax.random.fold_in(key, 11), 3)
    full_shape = (GRIDS, GRID, GRID, D)
    base_values = jnp.clip(jax.random.normal(key_base, full_shape, jnp.float32), -5.0, 5.0)
    row_scale = jnp.exp(jax.random.uniform(key_row, (GRIDS, GRID, GRID, 1), jnp.float32, math.log(0.3), math.log(3.0)))
    col_scale = jnp.exp(jax.random.uniform(key_col, (1, 1, 1, D), jnp.float32, math.log(0.5), math.log(2.0)))
    return (base_values * row_scale * col_scale).astype(jnp.bfloat16)


def draw_routing(key, part):
    n_devices = GRIDS * GRID * GRID // TOK_DEV
    rows_local = TOK_DEV // (GRIDS * GRID)
    group_size = EXPERTS // TOPK

    def one_block(block_key):
        sub_keys = jax.random.split(block_key, TOPK + 1)
        expert_order = jax.random.permutation(sub_keys[0], EXPERTS).astype(jnp.int32)
        columns = []
        for position in range(TOPK):
            token_ranks = jax.random.permutation(sub_keys[position + 1], TOK_DEV).astype(jnp.int32)
            columns.append(expert_order[position * group_size + token_ranks % group_size])
        return jnp.stack(columns, axis=1)
    all_blocks = jax.vmap(one_block)(jax.random.split(jax.random.fold_in(key, 7), n_devices))
    all_blocks = all_blocks.reshape(n_devices, GRIDS, rows_local, GRID, TOPK).transpose(1, 0, 2, 3, 4)
    return all_blocks.reshape(GRIDS, GRID, GRID, TOPK).astype(jnp.int32)


def shard_levels(rng, extent, shards, low, top_value):
    level = 1.0
    for dim, blocks in shards:
        heights = jax.random.uniform(jax.random.fold_in(jax.random.fold_in(rng, 6), dim), (blocks,), jnp.float32, low / len(shards), top_value / len(shards))
        level = level * jnp.repeat(jnp.exp(heights), extent[dim] // blocks).reshape((-1,) + (1,) * (len(extent) - 1 - dim))
    return level


def bell_draw(own_key, shape, scale, bound, pieces=(), held_as=jnp.bfloat16):
    result = jax.random.normal(own_key, shape, jnp.float32) * scale
    if len(pieces) > 0:
        result = shard_levels(own_key, shape, pieces, -0.22, 0.18) * result
    return jnp.clip(result, min=-bound, max=bound).astype(held_as)


def setup_inputs(seed: int = 0, part: int = 0) -> dict:
    keys = jax.random.split(jax.random.key(seed), 11)
    part_keys = jax.random.split(jax.random.fold_in(keys[10], part), 11)
    return {
        "tokens": draw_tokens(jax.random.fold_in(jax.random.fold_in(keys[10], part), 71), part),
        "ln_first": jnp.clip(1.0 + 0.1 * jax.random.normal(keys[1], (D,), jnp.float32), 0.5, 1.5),
        "spec_first": bell_draw(keys[2], (2, NB, D // NB, D // NB), (2 * D // NB) ** -0.5, 0.375),
        "spec_second": bell_draw(keys[3], (2, NB, D // NB, D // NB), (2 * D // NB) ** -0.5, 0.375),
        "spec_bias": bell_draw(keys[4], (2, D), 0.5, 3.0, (), jnp.float32),
        "ln_second": jnp.clip(1.0 + 0.1 * jax.random.normal(keys[5], (D,), jnp.float32), 0.5, 1.5),
        "routing": draw_routing(jax.random.fold_in(jax.random.fold_in(keys[10], part), 71), part),
        "combine": jnp.clip(0.1 + 0.5 * jax.random.uniform(part_keys[7], (GRIDS, GRID, GRID, TOPK), jnp.float32) ** shard_levels(part_keys[7], (GRIDS, GRID, GRID, TOPK), ((1, 16),), -0.2, 0.2), 0.1, 0.6),
        "up_weight": bell_draw(keys[8], (2 * EXPERTS, D, FF // 2), D ** -0.5, 0.1875, ((0, 8),)),
        "down_weight": bell_draw(keys[9], (2 * EXPERTS, FF // 2, D), FF ** -0.5, 0.109375, ((0, 8),)),
    }


def twiddle(length):
    counter = jnp.arange(length, dtype=jnp.float32)
    angle = 2.0 * math.pi / length * jnp.mod(jnp.outer(counter, counter), float(length))
    return (jnp.cos(angle), jnp.sin(angle))

def layer_norm(values, gain):
    values = values.astype(jnp.float32)
    center = values - lax.optimization_barrier(jnp.mean(values, axis=-1, keepdims=True))
    spread = lax.optimization_barrier(jnp.mean(center * center, axis=-1, keepdims=True))
    return center * lax.rsqrt(spread + 1e-05) * gain

def product(left, right, form):
    return jnp.einsum(form, left.astype(jnp.float32), right.astype(jnp.float32), precision=lax.Precision.HIGHEST)

def complex_blocks(real_in, imag_in, weight):
    form = 'ghkbi,bio->ghkbo'
    real_out = product(real_in, weight[0], form) - product(imag_in, weight[1], form)
    imag_out = product(real_in, weight[1], form) + product(imag_in, weight[0], form)
    return (real_out, imag_out)

def block_mlp(modes, first, second, bias):
    dims = modes.shape
    nblocks = first.shape[1]
    bwidth = first.shape[2]
    real_part = modes[:, 0].reshape(dims[0], dims[2], dims[3], nblocks, bwidth)
    imag_part = modes[:, 1].reshape(dims[0], dims[2], dims[3], nblocks, bwidth)
    hid_real, hid_imag = complex_blocks(real_part, imag_part, first)
    hid_real = jax.nn.relu(hid_real + bias[0].reshape(nblocks, bwidth)).astype(jnp.bfloat16)
    hid_imag = jax.nn.relu(hid_imag + bias[1].reshape(nblocks, bwidth)).astype(jnp.bfloat16)
    out_real, out_imag = complex_blocks(hid_real, hid_imag, second)
    return jnp.stack([out_real, out_imag], axis=1).reshape(dims).astype(jnp.bfloat16)

def reference(tokens, ln_first, spec_first, spec_second, spec_bias, ln_second, routing, combine, up_weight, down_weight):
    cosine, sine = twiddle(GRID)
    forward_cols = jnp.stack([cosine, -sine], axis=1).astype(jnp.bfloat16)
    forward_rows = jnp.stack([jnp.stack([cosine, sine], axis=1), jnp.stack([-sine, cosine], axis=1)], axis=0).astype(jnp.bfloat16)
    inverse_rows = jnp.stack([jnp.stack([cosine, -sine], axis=1), jnp.stack([sine, cosine], axis=1)], axis=0).astype(jnp.bfloat16)
    inverse_cols = jnp.stack([cosine, -sine], axis=0).astype(jnp.bfloat16)
    normed_first = layer_norm(tokens, ln_first).astype(jnp.bfloat16)
    col_spec = product(normed_first, forward_cols, 'ghwd,wck->gchkd').astype(jnp.bfloat16)
    modes = (product(forward_rows, col_spec, 'amch,gchkd->gamkd') * (1.0 / GRID)).astype(jnp.bfloat16)
    mixed_modes = block_mlp(modes, spec_first, spec_second, spec_bias)
    row_back = product(inverse_rows, mixed_modes, 'amch,gchkd->gamkd').astype(jnp.bfloat16)
    mixing = product(row_back, inverse_cols, 'gchkd,ckw->ghwd') * (1.0 / GRID)
    residual = (tokens.astype(jnp.float32) + mixing).astype(jnp.bfloat16)
    normed = layer_norm(residual, ln_second).astype(jnp.bfloat16).reshape(-1, D)
    flat_route = routing.reshape(-1).astype(jnp.int32)
    weights_flat = combine.reshape(-1)
    order_all = jnp.argsort(flat_route, stable=True).astype(jnp.int32).reshape(EXPERTS, -1)
    up_full = up_weight.reshape(EXPERTS, 2, D, FF // 2).transpose(0, 2, 1, 3).reshape(EXPERTS, D, FF)
    down_full = down_weight.reshape(EXPERTS, FF, D)

    def one_expert(inputs):
        picks, w_up, w_down = inputs
        rows_in = normed[picks // TOPK]
        hidden = jax.nn.gelu(jnp.dot(rows_in, w_up, preferred_element_type=jnp.float32), approximate=True).astype(jnp.bfloat16)
        return jnp.dot(hidden, w_down, preferred_element_type=jnp.float32) * weights_flat[picks][:, None]
    outputs = lax.map(one_expert, (order_all, up_full, down_full))
    total = jnp.zeros(normed.shape, jnp.float32).at[order_all.reshape(-1) // TOPK].add(outputs.reshape(-1, D))
    return (residual.astype(jnp.float32) + total.reshape(residual.shape)).astype(jnp.bfloat16)
```

```python
import math

import jax
import jax.numpy as jnp
import numpy as np
from jax import lax
from jax.experimental import pallas as pl
from jax.experimental.pallas import tpu as pltpu
from jax.sharding import Mesh
from jax.sharding import PartitionSpec as P


def from_partner(value, axis, stride):
    mask = 2**stride
    pairs = [(source, source ^ mask) for source in range(lax.axis_size(axis))]
    return lax.ppermute(value, axis, pairs)


def twiddle(length):
    counter = jnp.arange(length, dtype=jnp.float32)
    angle = 2.0 * math.pi / length * jnp.mod(jnp.outer(counter, counter), float(length))
    return (jnp.cos(angle), jnp.sin(angle))


def layer_norm(values, gain):
    values = values.astype(jnp.float32)
    center = values - jnp.mean(values, axis=-1, keepdims=True)
    spread = jnp.mean(center * center, axis=-1, keepdims=True)
    return center * lax.rsqrt(spread + 1e-05) * gain


def product(left, right, form):
    return jnp.einsum(form, left, right, preferred_element_type=jnp.float32)


def complex_blocks(real_in, imag_in, weight):
    form = "ghkbi,bio->ghkbo"
    real_out = product(real_in, weight[0], form) - product(imag_in, weight[1], form)
    imag_out = product(real_in, weight[1], form) + product(imag_in, weight[0], form)
    return (real_out, imag_out)


def block_mlp(modes, first, second, bias):
    dims = modes.shape
    nblocks = first.shape[1]
    bwidth = first.shape[2]
    real_part = modes[:, 0].reshape(dims[0], dims[2], dims[3], nblocks, bwidth)
    imag_part = modes[:, 1].reshape(dims[0], dims[2], dims[3], nblocks, bwidth)
    hid_real, hid_imag = complex_blocks(real_part, imag_part, first)
    hid_real = jax.nn.relu(hid_real + bias[0].reshape(nblocks, bwidth)).astype(jnp.bfloat16)
    hid_imag = jax.nn.relu(hid_imag + bias[1].reshape(nblocks, bwidth)).astype(jnp.bfloat16)
    out_real, out_imag = complex_blocks(hid_real, hid_imag, second)
    return jnp.stack([out_real, out_imag], axis=1).reshape(dims).astype(jnp.bfloat16)


def run_expert(arrived, up_full, down_full):
    in_shape = arrived.shape
    width = arrived.shape[2]
    hidden = jax.nn.gelu(
        jnp.dot(arrived.reshape(-1, width), up_full, preferred_element_type=jnp.float32),
        approximate=True,
    ).astype(jnp.bfloat16)
    partial_out = jnp.dot(hidden, down_full, preferred_element_type=jnp.float32).reshape(
        in_shape[0], in_shape[1], width
    )
    return lax.all_to_all(
        partial_out.astype(jnp.bfloat16), "row", split_axis=0, concat_axis=0, tiled=True
    ).astype(partial_out.dtype)


def per_device(
    tokens,
    ln_first,
    spec_first,
    spec_second,
    spec_bias,
    ln_second,
    routing,
    combine,
    up_weight,
    down_weight,
):
    grid_len = tokens.shape[2]
    width = tokens.shape[3]
    cosine, sine = twiddle(grid_len)
    forward_cols = jnp.stack([cosine, -sine], axis=1).astype(jnp.bfloat16)
    forward_rows = jnp.stack(
        [jnp.stack([cosine, sine], axis=1), jnp.stack([-sine, cosine], axis=1)], axis=0
    ).astype(jnp.bfloat16)
    inverse_rows = jnp.stack(
        [jnp.stack([cosine, -sine], axis=1), jnp.stack([sine, cosine], axis=1)], axis=0
    ).astype(jnp.bfloat16)
    inverse_cols = jnp.stack([cosine, -sine], axis=0).astype(jnp.bfloat16)
    normed_first = layer_norm(tokens, ln_first).astype(jnp.bfloat16)
    col_spec = product(normed_first, forward_cols, "ghwd,wck->gchkd").astype(jnp.bfloat16)
    by_column = lax.all_to_all(col_spec, ("row", "expert"), split_axis=3, concat_axis=2, tiled=True)
    modes = (product(forward_rows, by_column, "amch,gchkd->gamkd") * (1.0 / grid_len)).astype(
        jnp.bfloat16
    )
    mixed_modes = block_mlp(modes, spec_first, spec_second, spec_bias)
    row_back = product(inverse_rows, mixed_modes, "amch,gchkd->gamkd").astype(jnp.bfloat16)
    by_row = lax.all_to_all(row_back, ("row", "expert"), split_axis=2, concat_axis=3, tiled=True)
    mixing = product(by_row, inverse_cols, "gchkd,ckw->ghwd") * (1.0 / grid_len)
    residual = (tokens.astype(jnp.float32) + mixing).astype(jnp.bfloat16)
    normed = layer_norm(residual, ln_second).astype(jnp.bfloat16).reshape(-1, width)
    n_tokens = normed.shape[0]
    top_count = routing.shape[-1]
    experts = lax.axis_size("row") // 2
    capacity = n_tokens * top_count // experts
    flat_route = routing.reshape(-1)
    one_hot = (flat_route[:, None] == jnp.arange(experts, dtype=jnp.int32)[None, :]).astype(
        jnp.int32
    )
    earlier = jnp.cumsum(one_hot, axis=0) - one_hot
    slot_index = flat_route * capacity + jnp.sum(earlier * one_hot, axis=1)
    token_of = jnp.arange(n_tokens * top_count, dtype=jnp.int32) // top_count
    source_row = jnp.zeros((experts * capacity,), jnp.int32).at[slot_index].set(token_of)
    send_rows = normed[source_row].reshape(experts, capacity, width)
    partner_up, partner_down = from_partner((up_weight, down_weight), "row", 0)
    up_full = jnp.concatenate([up_weight[0], partner_up[0]], axis=1)
    down_full = jnp.concatenate([down_weight[0], partner_down[0]], axis=0)
    outgoing = send_rows.reshape(experts * 2, capacity // 2, width)
    returned = run_expert(
        lax.all_to_all(outgoing, "row", split_axis=0, concat_axis=0, tiled=True), up_full, down_full
    )
    results = returned.reshape(experts, capacity, width)
    gathered = results.reshape(-1, width)[slot_index].reshape(n_tokens, top_count, width)
    moe_out = jnp.sum(gathered * combine.reshape(n_tokens, top_count, 1), axis=1)
    final = residual.reshape(-1, width).astype(jnp.float32) + moe_out
    return final.reshape(tokens.shape).astype(jnp.bfloat16)


RING = ("ex", "half", "expert")


def mixer_kernel(slots, bwidth, scale, x_ref, d_ref, dt_ref, w1_ref, w2_ref, bias_ref, out_ref):
    rows, lanes = x_ref.shape
    grid_len = rows // (2 * slots)
    ranks = grid_len // 8
    x = x_ref[...].astype(jnp.float32).reshape(ranks, 2 * slots, 8, lanes)
    real_parts, imag_parts = [], []
    for slot in range(slots):
        pair = jnp.concatenate(
            [
                x[:, slot].reshape(grid_len, lanes),
                x[:, slots + slot].reshape(grid_len, lanes),
            ],
            axis=0,
        ).astype(jnp.bfloat16)
        modes = jnp.dot(d_ref[slot], pair, preferred_element_type=jnp.float32) * scale
        modes = modes.astype(jnp.bfloat16)
        real_parts.append(modes[: 2 * grid_len])
        imag_parts.append(modes[2 * grid_len :])
    real = jnp.concatenate(real_parts, axis=0)
    imag = jnp.concatenate(imag_parts, axis=0)
    mixed_real, mixed_imag = [], []
    for block in range(lanes // bwidth):
        cut = slice(block * bwidth, (block + 1) * bwidth)
        both = jnp.concatenate([real[:, cut], imag[:, cut]], axis=1)
        hid = jnp.dot(both, w1_ref[block], preferred_element_type=jnp.float32) + bias_ref[block]
        hid = jnp.maximum(hid, 0.0).astype(jnp.bfloat16)
        mixed = jnp.dot(hid, w2_ref[block], preferred_element_type=jnp.float32).astype(jnp.bfloat16)
        mixed_real.append(mixed[:, :bwidth])
        mixed_imag.append(mixed[:, bwidth:])
    real = jnp.concatenate(mixed_real, axis=1)
    imag = jnp.concatenate(mixed_imag, axis=1)
    back_real, back_imag = [], []
    for slot in range(slots):
        cut = slice(slot * 2 * grid_len, (slot + 1) * 2 * grid_len)
        column = jnp.concatenate([real[cut], imag[cut]], axis=0)
        back = jnp.dot(dt_ref[slot], column, preferred_element_type=jnp.float32)
        back_real.append(back[:grid_len].reshape(ranks, 8, lanes))
        back_imag.append(back[grid_len:].reshape(ranks, 8, lanes))
    out = jnp.stack(back_real + back_imag, axis=1).reshape(rows, lanes)
    out_ref[...] = out.astype(jnp.bfloat16)


def mixer(x, d, dt, w1, w2, bias, slots, scale):
    rows, width = x.shape
    nblocks, twice = w1.shape[:2]
    bwidth = twice // 2
    per_step = 2
    lanes = per_step * bwidth
    whole = lambda i: (0, 0, 0)
    weights = pl.BlockSpec((per_step, twice, twice), lambda i: (i, 0, 0))
    body = lambda *refs: mixer_kernel(slots, bwidth, scale, *refs)
    return pl.pallas_call(
        body,
        grid=(nblocks // per_step,),
        in_specs=[
            pl.BlockSpec((rows, lanes), lambda i: (0, i)),
            pl.BlockSpec(d.shape, whole),
            pl.BlockSpec(dt.shape, whole),
            weights,
            weights,
            pl.BlockSpec((per_step, 1, twice), lambda i: (i, 0, 0)),
        ],
        out_specs=pl.BlockSpec((rows, lanes), lambda i: (0, i)),
        out_shape=jax.ShapeDtypeStruct((rows, width), jnp.bfloat16),
        name="mixer",
    )(x, d, dt, w1, w2, bias)


def complex_square(weight):
    top = jnp.concatenate([weight[0], weight[1]], axis=2)
    low = jnp.concatenate([-weight[1], weight[0]], axis=2)
    return jnp.concatenate([top, low], axis=1)


def swap(value, mask):
    count = lax.axis_size("ex")
    return lax.ppermute(value, "ex", [(e, e ^ mask) for e in range(count)])


def expert_ffn(rows, up, down):
    total = None
    for part in range(up.shape[0]):
        hidden = jax.nn.gelu(
            jnp.dot(rows, up[part], preferred_element_type=jnp.float32), approximate=True
        ).astype(jnp.bfloat16)
        out = jnp.dot(hidden, down[part], preferred_element_type=jnp.float32)
        total = out if total is None else total + out
    return total


def per_device_dense(
    tokens,
    ln_first,
    spec_first,
    spec_second,
    spec_bias,
    ln_second,
    routing,
    combine,
    up_weight,
    down_weight,
):
    _, my_rows, grid_len, width = tokens.shape
    n_tokens = my_rows * grid_len
    ranks = grid_len // my_rows
    slots = grid_len // 2 // ranks
    experts = lax.axis_size("ex")
    copies = lax.axis_size("group") * lax.axis_size("expert")
    me = lax.axis_index(RING)
    my_expert = lax.axis_index("ex")

    share = lax.axis_index("group") * lax.axis_size("expert") + lax.axis_index("expert")
    up_rows = up_weight.shape[1] // copies
    down_rows = down_weight.shape[1] // copies
    up_piece = lax.dynamic_slice_in_dim(up_weight[0], share * up_rows, up_rows, 0)
    down_piece = lax.dynamic_slice_in_dim(down_weight[0], share * down_rows, down_rows, 0)
    held = []
    for mask in range(0, experts, 2):
        piece_up = up_piece if mask == 0 else swap(up_piece, mask)
        piece_down = down_piece if mask == 0 else swap(down_piece, mask)
        names = ("half", "group", "expert")
        full_up = lax.all_gather(piece_up, names, axis=0, tiled=True)
        full_down = lax.all_gather(piece_down, names, axis=0, tiled=True)
        held.append(
            (
                full_up.reshape((2,) + up_weight.shape[1:]),
                full_down.reshape((2,) + down_weight.shape[1:]),
            )
        )

    route = routing.reshape(n_tokens, -1)
    gate = combine.reshape(n_tokens, -1)
    by_expert = jnp.stack(
        [jnp.sum(jnp.where(route == e, gate, 0.0), axis=1) for e in range(experts)], axis=0
    )
    by_expert_other = swap(by_expert, 1)

    cosine, sine = twiddle(grid_len)
    half = grid_len // 2
    first_col = (jnp.arange(half) == 0)[:, None]
    packed = jnp.stack(
        [cosine[:half], jnp.where(first_col, cosine[half][None], -sine[:half])], axis=0
    ).astype(jnp.bfloat16)
    packed = packed.reshape(2, ranks, slots, grid_len).transpose(1, 0, 2, 3)
    eye = jnp.eye(my_rows, dtype=jnp.bfloat16)
    columns = (packed[:, :, :, None, None, :] * eye[None, None, None, :, :, None]).reshape(
        n_tokens, n_tokens
    )
    normed_first = layer_norm(tokens, ln_first).astype(jnp.bfloat16).reshape(n_tokens, width)
    col_spec = jnp.dot(columns, normed_first, preferred_element_type=jnp.float32)
    col_spec = col_spec.astype(jnp.bfloat16)
    by_column = lax.all_to_all(col_spec, RING, split_axis=0, concat_axis=0, tiled=True)

    none = jnp.zeros_like(cosine)
    usual = jnp.concatenate(
        [
            jnp.concatenate([cosine, sine], axis=1),
            jnp.concatenate([cosine, -sine], axis=1),
            jnp.concatenate([-sine, cosine], axis=1),
            jnp.concatenate([-sine, -cosine], axis=1),
        ],
        axis=0,
    )
    real_pair = jnp.concatenate(
        [
            jnp.concatenate([cosine, none], axis=1),
            jnp.concatenate([none, cosine], axis=1),
            jnp.concatenate([-sine, none], axis=1),
            jnp.concatenate([none, -sine], axis=1),
        ],
        axis=0,
    )
    is_first = ((jnp.arange(slots) == 0) & (me == 0))[:, None, None]
    rows_matrix = jnp.where(is_first, real_pair[None], usual[None]).astype(jnp.bfloat16)
    nblocks, bwidth = spec_first.shape[1:3]
    bias = jnp.concatenate(
        [spec_bias[0].reshape(nblocks, 1, bwidth), spec_bias[1].reshape(nblocks, 1, bwidth)], axis=2
    )
    row_back = mixer(
        by_column,
        rows_matrix,
        rows_matrix.transpose(0, 2, 1),
        complex_square(spec_first),
        complex_square(spec_second),
        bias,
        slots,
        1.0 / grid_len,
    )
    by_row = lax.all_to_all(row_back, RING, split_axis=0, concat_axis=0, tiled=True)
    mixing = lax.dot_general(
        columns, by_row, (((0,), (0,)), ((), ())), preferred_element_type=jnp.float32
    ) * (1.0 / grid_len)
    residual = (tokens.reshape(n_tokens, width).astype(jnp.float32) + mixing).astype(jnp.bfloat16)
    normed = layer_norm(residual, ln_second).astype(jnp.bfloat16)

    pieces = CHUNKS
    step = n_tokens // pieces
    arrived = [swap(normed[p * step : (p + 1) * step], 1) for p in range(pieces)]

    def weighted(rows, gates, index):
        expert = my_expert ^ (2 * index)
        gate_row = lax.dynamic_index_in_dim(gates, expert, axis=0, keepdims=False)
        return gate_row[:, None] * expert_ffn(rows, *held[index])

    own = residual.astype(jnp.float32)
    for index in range(len(held)):
        own = own + weighted(normed, by_expert, index)
    returned = []
    for p in range(pieces):
        gates = by_expert_other[:, p * step : (p + 1) * step]
        total = weighted(arrived[p], gates, 0)
        for index in range(1, len(held)):
            total = total + weighted(arrived[p], gates, index)
        returned.append(swap(total.astype(jnp.bfloat16), 1))
    final = own + jnp.concatenate(returned, axis=0).astype(jnp.float32)
    return final.reshape(tokens.shape).astype(jnp.bfloat16)


CHUNKS = 2


def solution(mesh):
    shape = mesh.shape
    group, row, expert = shape["group"], shape["row"], shape["expert"]
    split = Mesh(
        np.asarray(mesh.devices).reshape(group, row // 2, 2, expert),
        ("group", "ex", "half", "expert"),
    )

    def placed(row_names):
        cells = P("group", row_names + ("expert",), None, None)
        weights = P(row_names, None, None)
        return (cells, P(), P(), P(), P(), P(), cells, cells, weights, weights), cells

    def run(*args):
        experts = row // 2
        tokens, routing = args[0], args[6]
        ranks = row * expert
        dense = routing.shape[-1] == experts and experts % 4 == 0
        dense = dense and tokens.shape[1] == 8 * ranks and (tokens.shape[2] // 2) % ranks == 0
        dense = dense and tokens.shape[0] == group and args[8].shape[1] % (group * expert) == 0
        if dense:
            ins, outs = placed(("ex", "half"))
            call = jax.shard_map(
                per_device_dense, mesh=split, in_specs=ins, out_specs=outs, check_vma=False
            )
        else:
            ins, outs = placed(("row",))
            call = jax.shard_map(per_device, mesh=mesh, in_specs=ins, out_specs=outs, check_vma=False)
        return call(*args)

    return run
```

```python
import math

import jax
import jax.numpy as jnp
import numpy as np
from jax import lax
from jax.experimental import pallas as pl
from jax.experimental.pallas import tpu as pltpu
from jax.sharding import Mesh
from jax.sharding import PartitionSpec as P


def from_partner(value, axis, stride):
    mask = 2**stride
    pairs = [(source, source ^ mask) for source in range(lax.axis_size(axis))]
    return lax.ppermute(value, axis, pairs)


def twiddle(length):
    counter = jnp.arange(length, dtype=jnp.float32)
    angle = 2.0 * math.pi / length * jnp.mod(jnp.outer(counter, counter), float(length))
    return (jnp.cos(angle), jnp.sin(angle))


def layer_norm(values, gain):
    values = values.astype(jnp.float32)
    center = values - jnp.mean(values, axis=-1, keepdims=True)
    spread = jnp.mean(center * center, axis=-1, keepdims=True)
    return center * lax.rsqrt(spread + 1e-05) * gain


def product(left, right, form):
    return jnp.einsum(form, left, right, preferred_element_type=jnp.float32)


def complex_blocks(real_in, imag_in, weight):
    form = "ghkbi,bio->ghkbo"
    real_out = product(real_in, weight[0], form) - product(imag_in, weight[1], form)
    imag_out = product(real_in, weight[1], form) + product(imag_in, weight[0], form)
    return (real_out, imag_out)


def block_mlp(modes, first, second, bias):
    dims = modes.shape
    nblocks = first.shape[1]
    bwidth = first.shape[2]
    real_part = modes[:, 0].reshape(dims[0], dims[2], dims[3], nblocks, bwidth)
    imag_part = modes[:, 1].reshape(dims[0], dims[2], dims[3], nblocks, bwidth)
    hid_real, hid_imag = complex_blocks(real_part, imag_part, first)
    hid_real = jax.nn.relu(hid_real + bias[0].reshape(nblocks, bwidth)).astype(jnp.bfloat16)
    hid_imag = jax.nn.relu(hid_imag + bias[1].reshape(nblocks, bwidth)).astype(jnp.bfloat16)
    out_real, out_imag = complex_blocks(hid_real, hid_imag, second)
    return jnp.stack([out_real, out_imag], axis=1).reshape(dims).astype(jnp.bfloat16)


def run_expert(arrived, up_full, down_full):
    in_shape = arrived.shape
    width = arrived.shape[2]
    hidden = jax.nn.gelu(
        jnp.dot(arrived.reshape(-1, width), up_full, preferred_element_type=jnp.float32),
        approximate=True,
    ).astype(jnp.bfloat16)
    partial_out = jnp.dot(hidden, down_full, preferred_element_type=jnp.float32).reshape(
        in_shape[0], in_shape[1], width
    )
    return lax.all_to_all(
        partial_out.astype(jnp.bfloat16), "row", split_axis=0, concat_axis=0, tiled=True
    ).astype(partial_out.dtype)


def per_device(
    tokens,
    ln_first,
    spec_first,
    spec_second,
    spec_bias,
    ln_second,
    routing,
    combine,
    up_weight,
    down_weight,
):
    grid_len = tokens.shape[2]
    width = tokens.shape[3]
    cosine, sine = twiddle(grid_len)
    forward_cols = jnp.stack([cosine, -sine], axis=1).astype(jnp.bfloat16)
    forward_rows = jnp.stack(
        [jnp.stack([cosine, sine], axis=1), jnp.stack([-sine, cosine], axis=1)], axis=0
    ).astype(jnp.bfloat16)
    inverse_rows = jnp.stack(
        [jnp.stack([cosine, -sine], axis=1), jnp.stack([sine, cosine], axis=1)], axis=0
    ).astype(jnp.bfloat16)
    inverse_cols = jnp.stack([cosine, -sine], axis=0).astype(jnp.bfloat16)
    normed_first = layer_norm(tokens, ln_first).astype(jnp.bfloat16)
    col_spec = product(normed_first, forward_cols, "ghwd,wck->gchkd").astype(jnp.bfloat16)
    by_column = lax.all_to_all(col_spec, ("row", "expert"), split_axis=3, concat_axis=2, tiled=True)
    modes = (product(forward_rows, by_column, "amch,gchkd->gamkd") * (1.0 / grid_len)).astype(
        jnp.bfloat16
    )
    mixed_modes = block_mlp(modes, spec_first, spec_second, spec_bias)
    row_back = product(inverse_rows, mixed_modes, "amch,gchkd->gamkd").astype(jnp.bfloat16)
    by_row = lax.all_to_all(row_back, ("row", "expert"), split_axis=2, concat_axis=3, tiled=True)
    mixing = product(by_row, inverse_cols, "gchkd,ckw->ghwd") * (1.0 / grid_len)
    residual = (tokens.astype(jnp.float32) + mixing).astype(jnp.bfloat16)
    normed = layer_norm(residual, ln_second).astype(jnp.bfloat16).reshape(-1, width)
    n_tokens = normed.shape[0]
    top_count = routing.shape[-1]
    experts = lax.axis_size("row") // 2
    capacity = n_tokens * top_count // experts
    flat_route = routing.reshape(-1)
    one_hot = (flat_route[:, None] == jnp.arange(experts, dtype=jnp.int32)[None, :]).astype(
        jnp.int32
    )
    earlier = jnp.cumsum(one_hot, axis=0) - one_hot
    slot_index = flat_route * capacity + jnp.sum(earlier * one_hot, axis=1)
    token_of = jnp.arange(n_tokens * top_count, dtype=jnp.int32) // top_count
    source_row = jnp.zeros((experts * capacity,), jnp.int32).at[slot_index].set(token_of)
    send_rows = normed[source_row].reshape(experts, capacity, width)
    partner_up, partner_down = from_partner((up_weight, down_weight), "row", 0)
    up_full = jnp.concatenate([up_weight[0], partner_up[0]], axis=1)
    down_full = jnp.concatenate([down_weight[0], partner_down[0]], axis=0)
    outgoing = send_rows.reshape(experts * 2, capacity // 2, width)
    returned = run_expert(
        lax.all_to_all(outgoing, "row", split_axis=0, concat_axis=0, tiled=True), up_full, down_full
    )
    results = returned.reshape(experts, capacity, width)
    gathered = results.reshape(-1, width)[slot_index].reshape(n_tokens, top_count, width)
    moe_out = jnp.sum(gathered * combine.reshape(n_tokens, top_count, 1), axis=1)
    final = residual.reshape(-1, width).astype(jnp.float32) + moe_out
    return final.reshape(tokens.shape).astype(jnp.bfloat16)


RING = ("pair", "parity", "half", "expert")


def mixer_kernel(slots, bwidth, scale, x_ref, d_ref, dt_ref, w1_ref, w2_ref, bias_ref, out_ref):
    rows, lanes = x_ref.shape
    grid_len = rows // (2 * slots)
    ranks = grid_len // 8
    x = x_ref[...].astype(jnp.float32).reshape(ranks, 2 * slots, 8, lanes)
    real_parts, imag_parts = [], []
    for slot in range(slots):
        pair = jnp.concatenate(
            [
                x[:, slot].reshape(grid_len, lanes),
                x[:, slots + slot].reshape(grid_len, lanes),
            ],
            axis=0,
        ).astype(jnp.bfloat16)
        modes = jnp.dot(d_ref[slot], pair, preferred_element_type=jnp.float32) * scale
        modes = modes.astype(jnp.bfloat16)
        real_parts.append(modes[: 2 * grid_len])
        imag_parts.append(modes[2 * grid_len :])
    real = jnp.concatenate(real_parts, axis=0)
    imag = jnp.concatenate(imag_parts, axis=0)
    mixed_real, mixed_imag = [], []
    for block in range(lanes // bwidth):
        cut = slice(block * bwidth, (block + 1) * bwidth)
        both = jnp.concatenate([real[:, cut], imag[:, cut]], axis=1)
        hid = jnp.dot(both, w1_ref[block], preferred_element_type=jnp.float32) + bias_ref[block]
        hid = jnp.maximum(hid, 0.0).astype(jnp.bfloat16)
        mixed = jnp.dot(hid, w2_ref[block], preferred_element_type=jnp.float32).astype(jnp.bfloat16)
        mixed_real.append(mixed[:, :bwidth])
        mixed_imag.append(mixed[:, bwidth:])
    real = jnp.concatenate(mixed_real, axis=1)
    imag = jnp.concatenate(mixed_imag, axis=1)
    back_real, back_imag = [], []
    for slot in range(slots):
        cut = slice(slot * 2 * grid_len, (slot + 1) * 2 * grid_len)
        column = jnp.concatenate([real[cut], imag[cut]], axis=0)
        back = jnp.dot(dt_ref[slot], column, preferred_element_type=jnp.float32)
        back_real.append(back[:grid_len].reshape(ranks, 8, lanes))
        back_imag.append(back[grid_len:].reshape(ranks, 8, lanes))
    out = jnp.stack(back_real + back_imag, axis=1).reshape(rows, lanes)
    out_ref[...] = out.astype(jnp.bfloat16)


def mixer(x, d, dt, w1, w2, bias, slots, scale):
    rows, width = x.shape
    nblocks, twice = w1.shape[:2]
    bwidth = twice // 2
    per_step = 2
    lanes = per_step * bwidth
    whole = lambda i: (0, 0, 0)
    weights = pl.BlockSpec((per_step, twice, twice), lambda i: (i, 0, 0))
    body = lambda *refs: mixer_kernel(slots, bwidth, scale, *refs)
    return pl.pallas_call(
        body,
        grid=(nblocks // per_step,),
        in_specs=[
            pl.BlockSpec((rows, lanes), lambda i: (0, i)),
            pl.BlockSpec(d.shape, whole),
            pl.BlockSpec(dt.shape, whole),
            weights,
            weights,
            pl.BlockSpec((per_step, 1, twice), lambda i: (i, 0, 0)),
        ],
        out_specs=pl.BlockSpec((rows, lanes), lambda i: (0, i)),
        out_shape=jax.ShapeDtypeStruct((rows, width), jnp.bfloat16),
        name="mixer",
    )(x, d, dt, w1, w2, bias)


def complex_square(weight):
    top = jnp.concatenate([weight[0], weight[1]], axis=2)
    low = jnp.concatenate([-weight[1], weight[0]], axis=2)
    return jnp.concatenate([top, low], axis=1)


def swap(value):
    return lax.ppermute(value, "parity", [(0, 1), (1, 0)])


def ffn_kernel(steps, x_ref, gate_ref, up_ref, down_ref, out_ref, part_ref, total_ref):
    expert, step = pl.program_id(0), pl.program_id(1)
    rows = x_ref.shape[0]
    block = min(rows, 256)
    for start in range(0, rows, block):
        cut = pl.ds(start, block)
        hidden = jax.nn.gelu(
            jnp.dot(x_ref[cut, :], up_ref[0], preferred_element_type=jnp.float32), approximate=True
        ).astype(jnp.bfloat16)
        out = jnp.dot(hidden, down_ref[0], preferred_element_type=jnp.float32)

        @pl.when(step == 0)
        def _():
            part_ref[cut, :] = out

        @pl.when(step > 0)
        def _():
            part_ref[cut, :] = part_ref[cut, :] + out

    @pl.when(step == steps - 1)
    def _():
        lane = lax.broadcasted_iota(jnp.int32, gate_ref.shape, 1)
        gate = jnp.sum(jnp.where(lane == expert, gate_ref[...], 0.0), axis=1, keepdims=True)
        add = gate * part_ref[...]

        @pl.when(expert == 0)
        def _():
            total_ref[...] = add

        @pl.when(expert > 0)
        def _():
            total_ref[...] = total_ref[...] + add

        @pl.when(expert == pl.num_programs(0) - 1)
        def _():
            out_ref[...] = total_ref[...].astype(out_ref.dtype)


def expert_ffn(rows, gates, up, down, dtype):
    count, width = rows.shape
    experts = gates.shape[1]
    halves, _, hidden = up.shape
    cuts = 2
    chunk = hidden // cuts
    per = halves // experts
    steps = per * cuts
    return pl.pallas_call(
        lambda *refs: ffn_kernel(steps, *refs),
        grid=(experts, steps),
        in_specs=[
            pl.BlockSpec((count, width), lambda e, j: (0, 0)),
            pl.BlockSpec((count, experts), lambda e, j: (0, 0)),
            pl.BlockSpec((1, width, chunk), lambda e, j: (e * per + j // cuts, 0, j % cuts)),
            pl.BlockSpec((1, chunk, width), lambda e, j: (e * per + j // cuts, j % cuts, 0)),
        ],
        out_specs=pl.BlockSpec((count, width), lambda e, j: (0, 0)),
        out_shape=jax.ShapeDtypeStruct((count, width), dtype),
        scratch_shapes=[
            pltpu.VMEM((count, width), jnp.float32),
            pltpu.VMEM((count, width), jnp.float32),
        ],
        name="ffn",
    )(rows, gates, up, down)


def per_device_dense(
    tokens,
    ln_first,
    spec_first,
    spec_second,
    spec_bias,
    ln_second,
    routing,
    combine,
    up_weight,
    down_weight,
):
    _, my_rows, grid_len, width = tokens.shape
    n_tokens = my_rows * grid_len
    ranks = grid_len // my_rows
    slots = grid_len // 2 // ranks
    pairs = lax.axis_size("pair")
    copies = lax.axis_size("group") * lax.axis_size("expert")
    me = lax.axis_index(RING)
    parity = lax.axis_index("parity")

    share = lax.axis_index("group") * lax.axis_size("expert") + lax.axis_index("expert")
    up_rows = up_weight.shape[1] // copies
    down_rows = down_weight.shape[1] // copies
    up_piece = lax.dynamic_slice_in_dim(up_weight[0], share * up_rows, up_rows, 0)
    down_piece = lax.dynamic_slice_in_dim(down_weight[0], share * down_rows, down_rows, 0)
    names = ("pair", "half", "group", "expert")
    up_all = lax.all_gather(up_piece, names, axis=0, tiled=True)
    down_all = lax.all_gather(down_piece, names, axis=0, tiled=True)
    up_all = up_all.reshape((2 * pairs,) + up_weight.shape[1:])
    down_all = down_all.reshape((2 * pairs,) + down_weight.shape[1:])

    route = routing.reshape(n_tokens, -1)
    gate = combine.reshape(n_tokens, -1)

    def gates_for(side):
        return jnp.stack(
            [jnp.sum(jnp.where(route == 2 * e + side, gate, 0.0), axis=1) for e in range(pairs)]
        )

    own_gates = gates_for(parity).T
    other_gates = swap(gates_for(1 - parity))

    cosine, sine = twiddle(grid_len)
    half = grid_len // 2
    first_col = (jnp.arange(half) == 0)[:, None]
    packed = jnp.stack(
        [cosine[:half], jnp.where(first_col, cosine[half][None], -sine[:half])], axis=0
    ).astype(jnp.bfloat16)
    packed = packed.reshape(2, ranks, slots, grid_len).transpose(1, 0, 2, 3)
    eye = jnp.eye(my_rows, dtype=jnp.bfloat16)
    columns = (packed[:, :, :, None, None, :] * eye[None, None, None, :, :, None]).reshape(
        n_tokens, n_tokens
    )
    normed_first = layer_norm(tokens, ln_first).astype(jnp.bfloat16).reshape(n_tokens, width)
    col_spec = jnp.dot(columns, normed_first, preferred_element_type=jnp.float32)
    col_spec = col_spec.astype(jnp.bfloat16)
    col_spec, other_gates = lax.optimization_barrier((col_spec, other_gates))
    other_gates = other_gates.T
    by_column = lax.all_to_all(col_spec, RING, split_axis=0, concat_axis=0, tiled=True)

    none = jnp.zeros_like(cosine)
    usual = jnp.concatenate(
        [
            jnp.concatenate([cosine, sine], axis=1),
            jnp.concatenate([cosine, -sine], axis=1),
            jnp.concatenate([-sine, cosine], axis=1),
            jnp.concatenate([-sine, -cosine], axis=1),
        ],
        axis=0,
    )
    real_pair = jnp.concatenate(
        [
            jnp.concatenate([cosine, none], axis=1),
            jnp.concatenate([none, cosine], axis=1),
            jnp.concatenate([-sine, none], axis=1),
            jnp.concatenate([none, -sine], axis=1),
        ],
        axis=0,
    )
    is_first = ((jnp.arange(slots) == 0) & (me == 0))[:, None, None]
    rows_matrix = jnp.where(is_first, real_pair[None], usual[None]).astype(jnp.bfloat16)
    nblocks, bwidth = spec_first.shape[1:3]
    bias = jnp.concatenate(
        [spec_bias[0].reshape(nblocks, 1, bwidth), spec_bias[1].reshape(nblocks, 1, bwidth)], axis=2
    )
    row_back = mixer(
        by_column,
        rows_matrix,
        rows_matrix.transpose(0, 2, 1),
        complex_square(spec_first),
        complex_square(spec_second),
        bias,
        slots,
        1.0 / grid_len,
    )
    by_row = lax.all_to_all(row_back, RING, split_axis=0, concat_axis=0, tiled=True)
    mixing = lax.dot_general(
        columns, by_row, (((0,), (0,)), ((), ())), preferred_element_type=jnp.float32
    ) * (1.0 / grid_len)
    residual = (tokens.reshape(n_tokens, width).astype(jnp.float32) + mixing).astype(jnp.bfloat16)
    normed = layer_norm(residual, ln_second).astype(jnp.bfloat16)

    step = n_tokens // 2
    near, far = normed[:step], normed[step:]
    first_in, second_in = swap(near), swap(far)
    own_first = expert_ffn(near, own_gates[:step], up_all, down_all, jnp.float32)
    first_in, own_first = lax.optimization_barrier((first_in, own_first))
    first_out = expert_ffn(first_in, other_gates[:step], up_all, down_all, jnp.bfloat16)
    first_back = swap(first_out)
    second_in, first_out = lax.optimization_barrier((second_in, first_out))
    second_out = expert_ffn(second_in, other_gates[step:], up_all, down_all, jnp.bfloat16)
    second_back = swap(second_out)
    far, second_out = lax.optimization_barrier((far, second_out))
    own_second = expert_ffn(far, own_gates[step:], up_all, down_all, jnp.float32)
    own = jnp.concatenate([own_first, own_second], axis=0)
    back = jnp.concatenate([first_back, second_back], axis=0)
    final = residual.astype(jnp.float32) + own + back.astype(jnp.float32)
    return final.reshape(tokens.shape).astype(jnp.bfloat16)


def solution(mesh):
    shape = mesh.shape
    group, row, expert = shape["group"], shape["row"], shape["expert"]
    def placed(row_names):
        cells = P("group", row_names + ("expert",), None, None)
        weights = P(row_names, None, None)
        return (cells, P(), P(), P(), P(), P(), cells, cells, weights, weights), cells

    def run(*args):
        experts = row // 2
        tokens, routing = args[0], args[6]
        ranks = row * expert
        dense = routing.shape[-1] == experts and experts % 4 == 0
        dense = dense and tokens.shape[1] == 8 * ranks and (tokens.shape[2] // 2) % ranks == 0
        dense = dense and tokens.shape[0] == group and args[8].shape[1] % (group * expert) == 0
        if dense:
            split = Mesh(
                np.asarray(mesh.devices).reshape(group, row // 4, 2, 2, expert),
                ("group", "pair", "parity", "half", "expert"),
            )
            ins, outs = placed(("pair", "parity", "half"))
            call = jax.shard_map(
                per_device_dense, mesh=split, in_specs=ins, out_specs=outs, check_vma=False
            )
        else:
            ins, outs = placed(("row",))
            call = jax.shard_map(per_device, mesh=mesh, in_specs=ins, out_specs=outs, check_vma=False)
        return call(*args)

    return run
```

```python
import math

import jax
import jax.numpy as jnp
import numpy as np
from jax import lax
from jax.experimental import pallas as pl
from jax.experimental.pallas import tpu as pltpu
from jax.sharding import Mesh
from jax.sharding import PartitionSpec as P


def from_partner(value, axis, stride):
    mask = 2**stride
    pairs = [(source, source ^ mask) for source in range(lax.axis_size(axis))]
    return lax.ppermute(value, axis, pairs)


def twiddle(length):
    counter = jnp.arange(length, dtype=jnp.float32)
    angle = 2.0 * math.pi / length * jnp.mod(jnp.outer(counter, counter), float(length))
    return (jnp.cos(angle), jnp.sin(angle))


def layer_norm(values, gain):
    values = values.astype(jnp.float32)
    center = values - jnp.mean(values, axis=-1, keepdims=True)
    spread = jnp.mean(center * center, axis=-1, keepdims=True)
    return center * lax.rsqrt(spread + 1e-05) * gain


def product(left, right, form):
    return jnp.einsum(form, left, right, preferred_element_type=jnp.float32)


def complex_blocks(real_in, imag_in, weight):
    form = "ghkbi,bio->ghkbo"
    real_out = product(real_in, weight[0], form) - product(imag_in, weight[1], form)
    imag_out = product(real_in, weight[1], form) + product(imag_in, weight[0], form)
    return (real_out, imag_out)


def block_mlp(modes, first, second, bias):
    dims = modes.shape
    nblocks = first.shape[1]
    bwidth = first.shape[2]
    real_part = modes[:, 0].reshape(dims[0], dims[2], dims[3], nblocks, bwidth)
    imag_part = modes[:, 1].reshape(dims[0], dims[2], dims[3], nblocks, bwidth)
    hid_real, hid_imag = complex_blocks(real_part, imag_part, first)
    hid_real = jax.nn.relu(hid_real + bias[0].reshape(nblocks, bwidth)).astype(jnp.bfloat16)
    hid_imag = jax.nn.relu(hid_imag + bias[1].reshape(nblocks, bwidth)).astype(jnp.bfloat16)
    out_real, out_imag = complex_blocks(hid_real, hid_imag, second)
    return jnp.stack([out_real, out_imag], axis=1).reshape(dims).astype(jnp.bfloat16)


def run_expert(arrived, up_full, down_full):
    in_shape = arrived.shape
    width = arrived.shape[2]
    hidden = jax.nn.gelu(
        jnp.dot(arrived.reshape(-1, width), up_full, preferred_element_type=jnp.float32),
        approximate=True,
    ).astype(jnp.bfloat16)
    partial_out = jnp.dot(hidden, down_full, preferred_element_type=jnp.float32).reshape(
        in_shape[0], in_shape[1], width
    )
    return lax.all_to_all(
        partial_out.astype(jnp.bfloat16), "row", split_axis=0, concat_axis=0, tiled=True
    ).astype(partial_out.dtype)


def per_device(
    tokens,
    ln_first,
    spec_first,
    spec_second,
    spec_bias,
    ln_second,
    routing,
    combine,
    up_weight,
    down_weight,
):
    grid_len = tokens.shape[2]
    width = tokens.shape[3]
    cosine, sine = twiddle(grid_len)
    forward_cols = jnp.stack([cosine, -sine], axis=1).astype(jnp.bfloat16)
    forward_rows = jnp.stack(
        [jnp.stack([cosine, sine], axis=1), jnp.stack([-sine, cosine], axis=1)], axis=0
    ).astype(jnp.bfloat16)
    inverse_rows = jnp.stack(
        [jnp.stack([cosine, -sine], axis=1), jnp.stack([sine, cosine], axis=1)], axis=0
    ).astype(jnp.bfloat16)
    inverse_cols = jnp.stack([cosine, -sine], axis=0).astype(jnp.bfloat16)
    normed_first = layer_norm(tokens, ln_first).astype(jnp.bfloat16)
    col_spec = product(normed_first, forward_cols, "ghwd,wck->gchkd").astype(jnp.bfloat16)
    by_column = lax.all_to_all(col_spec, ("row", "expert"), split_axis=3, concat_axis=2, tiled=True)
    modes = (product(forward_rows, by_column, "amch,gchkd->gamkd") * (1.0 / grid_len)).astype(
        jnp.bfloat16
    )
    mixed_modes = block_mlp(modes, spec_first, spec_second, spec_bias)
    row_back = product(inverse_rows, mixed_modes, "amch,gchkd->gamkd").astype(jnp.bfloat16)
    by_row = lax.all_to_all(row_back, ("row", "expert"), split_axis=2, concat_axis=3, tiled=True)
    mixing = product(by_row, inverse_cols, "gchkd,ckw->ghwd") * (1.0 / grid_len)
    residual = (tokens.astype(jnp.float32) + mixing).astype(jnp.bfloat16)
    normed = layer_norm(residual, ln_second).astype(jnp.bfloat16).reshape(-1, width)
    n_tokens = normed.shape[0]
    top_count = routing.shape[-1]
    experts = lax.axis_size("row") // 2
    capacity = n_tokens * top_count // experts
    flat_route = routing.reshape(-1)
    one_hot = (flat_route[:, None] == jnp.arange(experts, dtype=jnp.int32)[None, :]).astype(
        jnp.int32
    )
    earlier = jnp.cumsum(one_hot, axis=0) - one_hot
    slot_index = flat_route * capacity + jnp.sum(earlier * one_hot, axis=1)
    token_of = jnp.arange(n_tokens * top_count, dtype=jnp.int32) // top_count
    source_row = jnp.zeros((experts * capacity,), jnp.int32).at[slot_index].set(token_of)
    send_rows = normed[source_row].reshape(experts, capacity, width)
    partner_up, partner_down = from_partner((up_weight, down_weight), "row", 0)
    up_full = jnp.concatenate([up_weight[0], partner_up[0]], axis=1)
    down_full = jnp.concatenate([down_weight[0], partner_down[0]], axis=0)
    outgoing = send_rows.reshape(experts * 2, capacity // 2, width)
    returned = run_expert(
        lax.all_to_all(outgoing, "row", split_axis=0, concat_axis=0, tiled=True), up_full, down_full
    )
    results = returned.reshape(experts, capacity, width)
    gathered = results.reshape(-1, width)[slot_index].reshape(n_tokens, top_count, width)
    moe_out = jnp.sum(gathered * combine.reshape(n_tokens, top_count, 1), axis=1)
    final = residual.reshape(-1, width).astype(jnp.float32) + moe_out
    return final.reshape(tokens.shape).astype(jnp.bfloat16)


RING = ("pair", "parity", "half", "expert")


def mixer_kernel(slots, bwidth, scale, x_ref, d_ref, dt_ref, w1_ref, w2_ref, bias_ref, out_ref):
    rows, lanes = x_ref.shape
    grid_len = rows // (2 * slots)
    ranks = grid_len // 8
    x = x_ref[...].astype(jnp.float32).reshape(ranks, 2 * slots, 8, lanes)
    real_parts, imag_parts = [], []
    for slot in range(slots):
        pair = jnp.concatenate(
            [
                x[:, slot].reshape(grid_len, lanes),
                x[:, slots + slot].reshape(grid_len, lanes),
            ],
            axis=0,
        ).astype(jnp.bfloat16)
        modes = jnp.dot(d_ref[slot], pair, preferred_element_type=jnp.float32) * scale
        modes = modes.astype(jnp.bfloat16)
        real_parts.append(modes[: 2 * grid_len])
        imag_parts.append(modes[2 * grid_len :])
    real = jnp.concatenate(real_parts, axis=0)
    imag = jnp.concatenate(imag_parts, axis=0)
    mixed_real, mixed_imag = [], []
    for block in range(lanes // bwidth):
        cut = slice(block * bwidth, (block + 1) * bwidth)
        both = jnp.concatenate([real[:, cut], imag[:, cut]], axis=1)
        hid = jnp.dot(both, w1_ref[block], preferred_element_type=jnp.float32) + bias_ref[block]
        hid = jnp.maximum(hid, 0.0).astype(jnp.bfloat16)
        mixed = jnp.dot(hid, w2_ref[block], preferred_element_type=jnp.float32).astype(jnp.bfloat16)
        mixed_real.append(mixed[:, :bwidth])
        mixed_imag.append(mixed[:, bwidth:])
    real = jnp.concatenate(mixed_real, axis=1)
    imag = jnp.concatenate(mixed_imag, axis=1)
    back_real, back_imag = [], []
    for slot in range(slots):
        cut = slice(slot * 2 * grid_len, (slot + 1) * 2 * grid_len)
        column = jnp.concatenate([real[cut], imag[cut]], axis=0)
        back = jnp.dot(dt_ref[slot], column, preferred_element_type=jnp.float32)
        back_real.append(back[:grid_len].reshape(ranks, 8, lanes))
        back_imag.append(back[grid_len:].reshape(ranks, 8, lanes))
    out = jnp.stack(back_real + back_imag, axis=1).reshape(rows, lanes)
    out_ref[...] = out.astype(jnp.bfloat16)


def mixer(x, d, dt, w1, w2, bias, slots, scale):
    rows, width = x.shape
    nblocks, twice = w1.shape[:2]
    bwidth = twice // 2
    per_step = 2
    lanes = per_step * bwidth
    whole = lambda i: (0, 0, 0)
    weights = pl.BlockSpec((per_step, twice, twice), lambda i: (i, 0, 0))
    body = lambda *refs: mixer_kernel(slots, bwidth, scale, *refs)
    return pl.pallas_call(
        body,
        grid=(nblocks // per_step,),
        in_specs=[
            pl.BlockSpec((rows, lanes), lambda i: (0, i)),
            pl.BlockSpec(d.shape, whole),
            pl.BlockSpec(dt.shape, whole),
            weights,
            weights,
            pl.BlockSpec((per_step, 1, twice), lambda i: (i, 0, 0)),
        ],
        out_specs=pl.BlockSpec((rows, lanes), lambda i: (0, i)),
        out_shape=jax.ShapeDtypeStruct((rows, width), jnp.bfloat16),
        name="mixer",
    )(x, d, dt, w1, w2, bias)


def complex_square(weight):
    top = jnp.concatenate([weight[0], weight[1]], axis=2)
    low = jnp.concatenate([-weight[1], weight[0]], axis=2)
    return jnp.concatenate([top, low], axis=1)


def swap(value):
    return lax.ppermute(value, "parity", [(0, 1), (1, 0)])


def ffn_kernel(steps, has_base, x_ref, gate_ref, up_ref, down_ref, *rest):
    base_ref = rest[0] if has_base else None
    out_ref, part_ref = rest[-2:]
    step = pl.program_id(0)
    hidden = up_ref.shape[2]
    wide = COLUMNS if hidden % COLUMNS == 0 else hidden
    cuts = [pl.ds(start, wide) for start in range(0, hidden, wide)]

    def lift(cut):
        return jnp.dot(x_ref[...], up_ref[0, :, cut], preferred_element_type=jnp.float32)

    out, ahead = None, lift(cuts[0])
    for index, cut in enumerate(cuts):
        raw = ahead
        if index + 1 < len(cuts):
            ahead = lift(cuts[index + 1])
        active = jax.nn.gelu(raw, approximate=True).astype(jnp.bfloat16)
        part = jnp.dot(active, down_ref[0, cut, :], preferred_element_type=jnp.float32)
        out = part if out is None else out + part

    @pl.when(step == 0)
    def _():
        part_ref[...] = out

    @pl.when(step > 0)
    def _():
        part_ref[...] = part_ref[...] + out

    @pl.when(step == steps - 1)
    def _():
        total = gate_ref[...] * part_ref[...]
        if has_base:
            total = total + base_ref[...]
        out_ref[...] = total.astype(out_ref.dtype)


COLUMNS = 512


def expert_ffn(rows, gate, up, down, base, dtype):
    count, width = rows.shape
    halves, _, hidden = up.shape
    steps = halves
    extra = [] if base is None else [base]
    flat = pl.BlockSpec((count, width), lambda j: (0, 0))
    return pl.pallas_call(
        lambda *refs: ffn_kernel(steps, base is not None, *refs),
        grid=(steps,),
        in_specs=[
            flat,
            pl.BlockSpec((count, 1), lambda j: (0, 0)),
            pl.BlockSpec((1, width, hidden), lambda j: (j, 0, 0)),
            pl.BlockSpec((1, hidden, width), lambda j: (j, 0, 0)),
        ]
        + [flat for _ in extra],
        out_specs=flat,
        out_shape=jax.ShapeDtypeStruct((count, width), dtype),
        scratch_shapes=[pltpu.VMEM((count, width), jnp.float32)],
        name="ffn",
    )(rows, gate, up, down, *extra)


def per_device_dense(
    tokens,
    ln_first,
    spec_first,
    spec_second,
    spec_bias,
    ln_second,
    routing,
    combine,
    up_weight,
    down_weight,
):
    _, my_rows, grid_len, width = tokens.shape
    n_tokens = my_rows * grid_len
    ranks = grid_len // my_rows
    slots = grid_len // 2 // ranks
    pairs = lax.axis_size("pair")
    copies = lax.axis_size("group") * lax.axis_size("expert")
    me = lax.axis_index(RING)
    parity = lax.axis_index("parity")

    share = lax.axis_index("group") * lax.axis_size("expert") + lax.axis_index("expert")
    up_rows = up_weight.shape[1] // copies
    down_rows = down_weight.shape[1] // copies
    up_piece = lax.dynamic_slice_in_dim(up_weight[0], share * up_rows, up_rows, 0)
    down_piece = lax.dynamic_slice_in_dim(down_weight[0], share * down_rows, down_rows, 0)
    names = ("half", "group", "expert")

    def gather(piece, whole):
        full = lax.all_gather(piece, names, axis=0, tiled=True)
        return full.reshape((2,) + whole.shape[1:])

    def far_plane(value, hop):
        return lax.ppermute(value, "pair", [(p, p ^ hop) for p in range(pairs)])

    mine = lax.axis_index("pair")
    held = [(gather(up_piece, up_weight), gather(down_piece, down_weight))]

    route = routing.reshape(n_tokens, -1)
    gate = combine.reshape(n_tokens, -1)

    def gates_for(side, hop):
        expert = 2 * (mine ^ hop) + side
        return jnp.sum(jnp.where(route == expert, gate, 0.0), axis=1)

    own_gates = jnp.stack([gates_for(parity, hop) for hop in range(pairs)])
    other_gates = swap(jnp.stack([gates_for(1 - parity, hop) for hop in range(pairs)]))

    cosine, sine = twiddle(grid_len)
    half = grid_len // 2
    first_col = (jnp.arange(half) == 0)[:, None]
    packed = jnp.stack(
        [cosine[:half], jnp.where(first_col, cosine[half][None], -sine[:half])], axis=0
    ).astype(jnp.bfloat16)
    packed = packed.reshape(2, ranks, slots, grid_len).transpose(1, 0, 2, 3)
    eye = jnp.eye(my_rows, dtype=jnp.bfloat16)
    columns = (packed[:, :, :, None, None, :] * eye[None, None, None, :, :, None]).reshape(
        n_tokens, n_tokens
    )
    normed_first = layer_norm(tokens, ln_first).astype(jnp.bfloat16).reshape(n_tokens, width)
    col_spec = jnp.dot(columns, normed_first, preferred_element_type=jnp.float32)
    col_spec = col_spec.astype(jnp.bfloat16)
    col_spec, other_gates = lax.optimization_barrier((col_spec, other_gates))
    by_column = lax.all_to_all(col_spec, RING, split_axis=0, concat_axis=0, tiled=True)
    far_up = [far_plane(up_piece, hop) for hop in range(1, pairs)]
    by_column, far_up, down_piece = lax.optimization_barrier((by_column, far_up, down_piece))
    far_up = [gather(piece, up_weight) for piece in far_up]

    none = jnp.zeros_like(cosine)
    usual = jnp.concatenate(
        [
            jnp.concatenate([cosine, sine], axis=1),
            jnp.concatenate([cosine, -sine], axis=1),
            jnp.concatenate([-sine, cosine], axis=1),
            jnp.concatenate([-sine, -cosine], axis=1),
        ],
        axis=0,
    )
    real_pair = jnp.concatenate(
        [
            jnp.concatenate([cosine, none], axis=1),
            jnp.concatenate([none, cosine], axis=1),
            jnp.concatenate([-sine, none], axis=1),
            jnp.concatenate([none, -sine], axis=1),
        ],
        axis=0,
    )
    is_first = ((jnp.arange(slots) == 0) & (me == 0))[:, None, None]
    rows_matrix = jnp.where(is_first, real_pair[None], usual[None]).astype(jnp.bfloat16)
    nblocks, bwidth = spec_first.shape[1:3]
    bias = jnp.concatenate(
        [spec_bias[0].reshape(nblocks, 1, bwidth), spec_bias[1].reshape(nblocks, 1, bwidth)], axis=2
    )
    row_back = mixer(
        by_column,
        rows_matrix,
        rows_matrix.transpose(0, 2, 1),
        complex_square(spec_first),
        complex_square(spec_second),
        bias,
        slots,
        1.0 / grid_len,
    )
    by_row = lax.all_to_all(row_back, RING, split_axis=0, concat_axis=0, tiled=True)
    far_down = [far_plane(down_piece, hop) for hop in range(1, pairs)]
    by_row, far_down = lax.optimization_barrier((by_row, far_down))
    far_down = [gather(piece, down_weight) for piece in far_down]
    held += list(zip(far_up, far_down))
    mixing = lax.dot_general(
        columns, by_row, (((0,), (0,)), ((), ())), preferred_element_type=jnp.float32
    ) * (1.0 / grid_len)
    residual = (tokens.reshape(n_tokens, width).astype(jnp.float32) + mixing).astype(jnp.bfloat16)
    normed = layer_norm(residual, ln_second).astype(jnp.bfloat16)

    step = n_tokens // 2
    near, far = normed[:step], normed[step:]
    first_in, second_in = swap(near), swap(far)
    last = pairs - 1

    def run(rows, gates, start, index, base, dtype):
        column = gates[index, start : start + step][:, None]
        return expert_ffn(rows, column, *held[index], base, dtype)

    def after(value, other):
        return lax.optimization_barrier((value, other))

    wide = jnp.float32
    own_first = run(near, own_gates, 0, 0, None, wide)
    far, own_first = after(far, own_first)
    own_second = run(far, own_gates, step, 0, None, wide)
    first_in, own_second = after(first_in, own_second)
    first_out = run(first_in, other_gates, 0, 0, None, wide)
    second_in, first_out = after(second_in, first_out)
    second_out = run(second_in, other_gates, step, 0, None, wide)
    for index in range(1, pairs):
        kind = jnp.bfloat16 if index == last else wide
        first_in, second_out = after(first_in, second_out)
        first_out = run(first_in, other_gates, 0, index, first_out, kind)
        if index == last:
            first_back = swap(first_out)
        second_in, first_out = after(second_in, first_out)
        second_out = run(second_in, other_gates, step, index, second_out, kind)
        if index == last:
            second_back = swap(second_out)
        near, second_out = after(near, second_out)
        own_first = run(near, own_gates, 0, index, own_first, wide)
        far, own_first = after(far, own_first)
        own_second = run(far, own_gates, step, index, own_second, wide)
        first_in, own_second = after(first_in, own_second)
    own = jnp.concatenate([own_first, own_second], axis=0)
    back = jnp.concatenate([first_back, second_back], axis=0)
    final = residual.astype(jnp.float32) + own + back.astype(jnp.float32)
    return final.reshape(tokens.shape).astype(jnp.bfloat16)


def solution(mesh):
    shape = mesh.shape
    group, row, expert = shape["group"], shape["row"], shape["expert"]
    def placed(row_names):
        cells = P("group", row_names + ("expert",), None, None)
        weights = P(row_names, None, None)
        return (cells, P(), P(), P(), P(), P(), cells, cells, weights, weights), cells

    def run(*args):
        experts = row // 2
        tokens, routing = args[0], args[6]
        ranks = row * expert
        dense = routing.shape[-1] == experts and experts % 4 == 0
        dense = dense and tokens.shape[1] == 8 * ranks and (tokens.shape[2] // 2) % ranks == 0
        dense = dense and tokens.shape[0] == group and args[8].shape[1] % (group * expert) == 0
        if dense:
            split = Mesh(
                np.asarray(mesh.devices).reshape(group, row // 4, 2, 2, expert),
                ("group", "pair", "parity", "half", "expert"),
            )
            ins, outs = placed(("pair", "parity", "half"))
            call = jax.shard_map(
                per_device_dense, mesh=split, in_specs=ins, out_specs=outs, check_vma=False
            )
        else:
            ins, outs = placed(("row",))
            call = jax.shard_map(per_device, mesh=mesh, in_specs=ins, out_specs=outs, check_vma=False)
        return call(*args)

    return run
```

```python
import math

import jax
import jax.numpy as jnp
import numpy as np
from jax import lax
from jax.experimental import pallas as pl
from jax.experimental.pallas import tpu as pltpu
from jax.sharding import Mesh
from jax.sharding import PartitionSpec as P


def from_partner(value, axis, stride):
    mask = 2**stride
    pairs = [(source, source ^ mask) for source in range(lax.axis_size(axis))]
    return lax.ppermute(value, axis, pairs)


def twiddle(length):
    counter = jnp.arange(length, dtype=jnp.float32)
    angle = 2.0 * math.pi / length * jnp.mod(jnp.outer(counter, counter), float(length))
    return (jnp.cos(angle), jnp.sin(angle))


def layer_norm(values, gain):
    values = values.astype(jnp.float32)
    center = values - jnp.mean(values, axis=-1, keepdims=True)
    spread = jnp.mean(center * center, axis=-1, keepdims=True)
    return center * lax.rsqrt(spread + 1e-05) * gain


def product(left, right, form):
    return jnp.einsum(form, left, right, preferred_element_type=jnp.float32)


def complex_blocks(real_in, imag_in, weight):
    form = "ghkbi,bio->ghkbo"
    real_out = product(real_in, weight[0], form) - product(imag_in, weight[1], form)
    imag_out = product(real_in, weight[1], form) + product(imag_in, weight[0], form)
    return (real_out, imag_out)


def block_mlp(modes, first, second, bias):
    dims = modes.shape
    nblocks = first.shape[1]
    bwidth = first.shape[2]
    real_part = modes[:, 0].reshape(dims[0], dims[2], dims[3], nblocks, bwidth)
    imag_part = modes[:, 1].reshape(dims[0], dims[2], dims[3], nblocks, bwidth)
    hid_real, hid_imag = complex_blocks(real_part, imag_part, first)
    hid_real = jax.nn.relu(hid_real + bias[0].reshape(nblocks, bwidth)).astype(jnp.bfloat16)
    hid_imag = jax.nn.relu(hid_imag + bias[1].reshape(nblocks, bwidth)).astype(jnp.bfloat16)
    out_real, out_imag = complex_blocks(hid_real, hid_imag, second)
    return jnp.stack([out_real, out_imag], axis=1).reshape(dims).astype(jnp.bfloat16)


def run_expert(arrived, up_full, down_full):
    in_shape = arrived.shape
    width = arrived.shape[2]
    hidden = jax.nn.gelu(
        jnp.dot(arrived.reshape(-1, width), up_full, preferred_element_type=jnp.float32),
        approximate=True,
    ).astype(jnp.bfloat16)
    partial_out = jnp.dot(hidden, down_full, preferred_element_type=jnp.float32).reshape(
        in_shape[0], in_shape[1], width
    )
    return lax.all_to_all(
        partial_out.astype(jnp.bfloat16), "row", split_axis=0, concat_axis=0, tiled=True
    ).astype(partial_out.dtype)


def per_device(
    tokens,
    ln_first,
    spec_first,
    spec_second,
    spec_bias,
    ln_second,
    routing,
    combine,
    up_weight,
    down_weight,
):
    grid_len = tokens.shape[2]
    width = tokens.shape[3]
    cosine, sine = twiddle(grid_len)
    forward_cols = jnp.stack([cosine, -sine], axis=1).astype(jnp.bfloat16)
    forward_rows = jnp.stack(
        [jnp.stack([cosine, sine], axis=1), jnp.stack([-sine, cosine], axis=1)], axis=0
    ).astype(jnp.bfloat16)
    inverse_rows = jnp.stack(
        [jnp.stack([cosine, -sine], axis=1), jnp.stack([sine, cosine], axis=1)], axis=0
    ).astype(jnp.bfloat16)
    inverse_cols = jnp.stack([cosine, -sine], axis=0).astype(jnp.bfloat16)
    normed_first = layer_norm(tokens, ln_first).astype(jnp.bfloat16)
    col_spec = product(normed_first, forward_cols, "ghwd,wck->gchkd").astype(jnp.bfloat16)
    by_column = lax.all_to_all(col_spec, ("row", "expert"), split_axis=3, concat_axis=2, tiled=True)
    modes = (product(forward_rows, by_column, "amch,gchkd->gamkd") * (1.0 / grid_len)).astype(
        jnp.bfloat16
    )
    mixed_modes = block_mlp(modes, spec_first, spec_second, spec_bias)
    row_back = product(inverse_rows, mixed_modes, "amch,gchkd->gamkd").astype(jnp.bfloat16)
    by_row = lax.all_to_all(row_back, ("row", "expert"), split_axis=2, concat_axis=3, tiled=True)
    mixing = product(by_row, inverse_cols, "gchkd,ckw->ghwd") * (1.0 / grid_len)
    residual = (tokens.astype(jnp.float32) + mixing).astype(jnp.bfloat16)
    normed = layer_norm(residual, ln_second).astype(jnp.bfloat16).reshape(-1, width)
    n_tokens = normed.shape[0]
    top_count = routing.shape[-1]
    experts = lax.axis_size("row") // 2
    capacity = n_tokens * top_count // experts
    flat_route = routing.reshape(-1)
    one_hot = (flat_route[:, None] == jnp.arange(experts, dtype=jnp.int32)[None, :]).astype(
        jnp.int32
    )
    earlier = jnp.cumsum(one_hot, axis=0) - one_hot
    slot_index = flat_route * capacity + jnp.sum(earlier * one_hot, axis=1)
    token_of = jnp.arange(n_tokens * top_count, dtype=jnp.int32) // top_count
    source_row = jnp.zeros((experts * capacity,), jnp.int32).at[slot_index].set(token_of)
    send_rows = normed[source_row].reshape(experts, capacity, width)
    partner_up, partner_down = from_partner((up_weight, down_weight), "row", 0)
    up_full = jnp.concatenate([up_weight[0], partner_up[0]], axis=1)
    down_full = jnp.concatenate([down_weight[0], partner_down[0]], axis=0)
    outgoing = send_rows.reshape(experts * 2, capacity // 2, width)
    returned = run_expert(
        lax.all_to_all(outgoing, "row", split_axis=0, concat_axis=0, tiled=True), up_full, down_full
    )
    results = returned.reshape(experts, capacity, width)
    gathered = results.reshape(-1, width)[slot_index].reshape(n_tokens, top_count, width)
    moe_out = jnp.sum(gathered * combine.reshape(n_tokens, top_count, 1), axis=1)
    final = residual.reshape(-1, width).astype(jnp.float32) + moe_out
    return final.reshape(tokens.shape).astype(jnp.bfloat16)


RING = ("pair", "parity", "half", "expert")


def mixer_kernel(slots, bwidth, scale, x_ref, d_ref, dt_ref, w1_ref, w2_ref, bias_ref, out_ref):
    rows, lanes = x_ref.shape
    grid_len = rows // (2 * slots)
    ranks = grid_len // 8
    x = x_ref[...].astype(jnp.float32).reshape(ranks, 2 * slots, 8, lanes)
    real_parts, imag_parts = [], []
    for slot in range(slots):
        pair = jnp.concatenate(
            [
                x[:, slot].reshape(grid_len, lanes),
                x[:, slots + slot].reshape(grid_len, lanes),
            ],
            axis=0,
        ).astype(jnp.bfloat16)
        modes = jnp.dot(d_ref[slot], pair, preferred_element_type=jnp.float32) * scale
        modes = modes.astype(jnp.bfloat16)
        real_parts.append(modes[: 2 * grid_len])
        imag_parts.append(modes[2 * grid_len :])
    real = jnp.concatenate(real_parts, axis=0)
    imag = jnp.concatenate(imag_parts, axis=0)
    mixed_real, mixed_imag = [], []
    for block in range(lanes // bwidth):
        cut = slice(block * bwidth, (block + 1) * bwidth)
        both = jnp.concatenate([real[:, cut], imag[:, cut]], axis=1)
        hid = jnp.dot(both, w1_ref[block], preferred_element_type=jnp.float32) + bias_ref[block]
        hid = jnp.maximum(hid, 0.0).astype(jnp.bfloat16)
        mixed = jnp.dot(hid, w2_ref[block], preferred_element_type=jnp.float32).astype(jnp.bfloat16)
        mixed_real.append(mixed[:, :bwidth])
        mixed_imag.append(mixed[:, bwidth:])
    real = jnp.concatenate(mixed_real, axis=1)
    imag = jnp.concatenate(mixed_imag, axis=1)
    back_real, back_imag = [], []
    for slot in range(slots):
        cut = slice(slot * 2 * grid_len, (slot + 1) * 2 * grid_len)
        column = jnp.concatenate([real[cut], imag[cut]], axis=0)
        back = jnp.dot(dt_ref[slot], column, preferred_element_type=jnp.float32)
        back_real.append(back[:grid_len].reshape(ranks, 8, lanes))
        back_imag.append(back[grid_len:].reshape(ranks, 8, lanes))
    out = jnp.stack(back_real + back_imag, axis=1).reshape(rows, lanes)
    out_ref[...] = out.astype(jnp.bfloat16)


def mixer(x, d, dt, w1, w2, bias, slots, scale):
    rows, width = x.shape
    nblocks, twice = w1.shape[:2]
    bwidth = twice // 2
    per_step = 2
    lanes = per_step * bwidth
    whole = lambda i: (0, 0, 0)
    weights = pl.BlockSpec((per_step, twice, twice), lambda i: (i, 0, 0))
    body = lambda *refs: mixer_kernel(slots, bwidth, scale, *refs)
    return pl.pallas_call(
        body,
        grid=(nblocks // per_step,),
        in_specs=[
            pl.BlockSpec((rows, lanes), lambda i: (0, i)),
            pl.BlockSpec(d.shape, whole),
            pl.BlockSpec(dt.shape, whole),
            weights,
            weights,
            pl.BlockSpec((per_step, 1, twice), lambda i: (i, 0, 0)),
        ],
        out_specs=pl.BlockSpec((rows, lanes), lambda i: (0, i)),
        out_shape=jax.ShapeDtypeStruct((rows, width), jnp.bfloat16),
        name="mixer",
    )(x, d, dt, w1, w2, bias)


def complex_square(weight):
    top = jnp.concatenate([weight[0], weight[1]], axis=2)
    low = jnp.concatenate([-weight[1], weight[0]], axis=2)
    return jnp.concatenate([top, low], axis=1)


def swap(value):
    return lax.ppermute(value, "parity", [(0, 1), (1, 0)])


def ffn_kernel(steps, has_base, x_ref, gate_ref, up_ref, down_ref, *rest):
    base_ref = rest[0] if has_base else None
    out_ref, part_ref = rest[-2:]
    step = pl.program_id(1)
    hidden = up_ref.shape[2]
    wide = COLUMNS if hidden % COLUMNS == 0 else hidden
    cuts = [pl.ds(start, wide) for start in range(0, hidden, wide)]

    def lift(cut):
        return jnp.dot(x_ref[...], up_ref[0, :, cut], preferred_element_type=jnp.float32)

    out, ahead = None, lift(cuts[0])
    for index, cut in enumerate(cuts):
        raw = ahead
        if index + 1 < len(cuts):
            ahead = lift(cuts[index + 1])
        active = jax.nn.gelu(raw, approximate=True).astype(jnp.bfloat16)
        part = jnp.dot(active, down_ref[0, cut, :], preferred_element_type=jnp.float32)
        out = part if out is None else out + part

    @pl.when(step == 0)
    def _():
        part_ref[...] = out

    @pl.when(step > 0)
    def _():
        part_ref[...] = part_ref[...] + out

    @pl.when(step == steps - 1)
    def _():
        total = gate_ref[...] * part_ref[...]
        if has_base:
            total = total + base_ref[...]
        out_ref[...] = total.astype(out_ref.dtype)


COLUMNS = 512


def expert_ffn(rows, gate, up, down, base, block, dtype):
    count, width = rows.shape
    steps, _, hidden = up.shape
    extra = [] if base is None else [base]
    flat = pl.BlockSpec((block, width), lambda i, j: (i, 0))
    return pl.pallas_call(
        lambda *refs: ffn_kernel(steps, base is not None, *refs),
        grid=(count // block, steps),
        in_specs=[
            flat,
            pl.BlockSpec((block, 1), lambda i, j: (i, 0)),
            pl.BlockSpec((1, width, hidden), lambda i, j: (j, 0, 0)),
            pl.BlockSpec((1, hidden, width), lambda i, j: (j, 0, 0)),
        ]
        + [flat for _ in extra],
        out_specs=flat,
        out_shape=jax.ShapeDtypeStruct((count, width), dtype),
        scratch_shapes=[pltpu.VMEM((block, width), jnp.float32)],
        name="ffn",
    )(rows, gate, up, down, *extra)


def per_device_dense(
    tokens,
    ln_first,
    spec_first,
    spec_second,
    spec_bias,
    ln_second,
    routing,
    combine,
    up_weight,
    down_weight,
):
    _, my_rows, grid_len, width = tokens.shape
    n_tokens = my_rows * grid_len
    ranks = grid_len // my_rows
    slots = grid_len // 2 // ranks
    pairs = lax.axis_size("pair")
    copies = lax.axis_size("group") * lax.axis_size("expert")
    me = lax.axis_index(RING)
    parity = lax.axis_index("parity")

    share = lax.axis_index("group") * lax.axis_size("expert") + lax.axis_index("expert")
    up_rows = up_weight.shape[1] // copies
    down_rows = down_weight.shape[1] // copies
    up_piece = lax.dynamic_slice_in_dim(up_weight[0], share * up_rows, up_rows, 0)
    down_piece = lax.dynamic_slice_in_dim(down_weight[0], share * down_rows, down_rows, 0)
    names = ("half", "group", "expert")

    def gather(piece, whole):
        full = lax.all_gather(piece, names, axis=0, tiled=True)
        return full.reshape((2,) + whole.shape[1:])

    def far_plane(value, hop):
        return lax.ppermute(value, "pair", [(p, p ^ hop) for p in range(pairs)])

    mine = lax.axis_index("pair")
    held = [(gather(up_piece, up_weight), gather(down_piece, down_weight))]

    route = routing.reshape(n_tokens, -1)
    gate = combine.reshape(n_tokens, -1)

    def gates_for(side, hop):
        expert = 2 * (mine ^ hop) + side
        return jnp.sum(jnp.where(route == expert, gate, 0.0), axis=1)

    own_gates = jnp.stack([gates_for(parity, hop) for hop in range(pairs)])
    other_gates = swap(jnp.stack([gates_for(1 - parity, hop) for hop in range(pairs)]))

    cosine, sine = twiddle(grid_len)
    half = grid_len // 2
    first_col = (jnp.arange(half) == 0)[:, None]
    packed = jnp.stack(
        [cosine[:half], jnp.where(first_col, cosine[half][None], -sine[:half])], axis=0
    ).astype(jnp.bfloat16)
    packed = packed.reshape(2, ranks, slots, grid_len).transpose(1, 0, 2, 3)
    eye = jnp.eye(my_rows, dtype=jnp.bfloat16)
    columns = (packed[:, :, :, None, None, :] * eye[None, None, None, :, :, None]).reshape(
        n_tokens, n_tokens
    )
    normed_first = layer_norm(tokens, ln_first).astype(jnp.bfloat16).reshape(n_tokens, width)
    col_spec = jnp.dot(columns, normed_first, preferred_element_type=jnp.float32)
    col_spec = col_spec.astype(jnp.bfloat16)
    none = jnp.zeros_like(cosine)
    usual = jnp.concatenate(
        [
            jnp.concatenate([cosine, sine], axis=1),
            jnp.concatenate([cosine, -sine], axis=1),
            jnp.concatenate([-sine, cosine], axis=1),
            jnp.concatenate([-sine, -cosine], axis=1),
        ],
        axis=0,
    )
    real_pair = jnp.concatenate(
        [
            jnp.concatenate([cosine, none], axis=1),
            jnp.concatenate([none, cosine], axis=1),
            jnp.concatenate([-sine, none], axis=1),
            jnp.concatenate([none, -sine], axis=1),
        ],
        axis=0,
    )
    is_first = ((jnp.arange(slots) == 0) & (me == 0))[:, None, None]
    rows_matrix = jnp.where(is_first, real_pair[None], usual[None]).astype(jnp.bfloat16)
    nblocks, bwidth = spec_first.shape[1:3]
    bias = jnp.concatenate(
        [spec_bias[0].reshape(nblocks, 1, bwidth), spec_bias[1].reshape(nblocks, 1, bwidth)], axis=2
    )
    prepared = (
        rows_matrix,
        rows_matrix.transpose(0, 2, 1),
        complex_square(spec_first),
        complex_square(spec_second),
        bias,
    )
    col_spec, other_gates, prepared = lax.optimization_barrier((col_spec, other_gates, prepared))
    by_column = lax.all_to_all(col_spec, RING, split_axis=0, concat_axis=0, tiled=True)
    far_up = [far_plane(up_piece, hop) for hop in range(1, pairs)]
    by_column, far_up, down_piece = lax.optimization_barrier((by_column, far_up, down_piece))
    far_up = [gather(piece, up_weight) for piece in far_up]

    row_back = mixer(by_column, *prepared, slots, 1.0 / grid_len)
    by_row = lax.all_to_all(row_back, RING, split_axis=0, concat_axis=0, tiled=True)
    far_down = [far_plane(down_piece, hop) for hop in range(1, pairs)]
    by_row, far_down = lax.optimization_barrier((by_row, far_down))
    far_down = [gather(piece, down_weight) for piece in far_down]
    held += list(zip(far_up, far_down))
    mixing = lax.dot_general(
        columns, by_row, (((0,), (0,)), ((), ())), preferred_element_type=jnp.float32
    ) * (1.0 / grid_len)
    residual = (tokens.reshape(n_tokens, width).astype(jnp.float32) + mixing).astype(jnp.bfloat16)
    normed = layer_norm(residual, ln_second).astype(jnp.bfloat16)

    step = n_tokens // 2
    near, far = normed[:step], normed[step:]
    first_in, second_in = swap(near), swap(far)
    last = pairs - 1

    def run(rows, gates, index, base, dtype):
        return expert_ffn(rows, gates[index][:, None], *held[index], base, step, dtype)

    def after(value, other):
        return lax.optimization_barrier((value, other))

    wide = jnp.float32
    near_gates, far_gates = other_gates[:, :step], other_gates[:, step:]
    own = run(normed, own_gates, 0, None, wide)
    first_in, own = after(first_in, own)
    first_out = run(first_in, near_gates, 0, None, wide)
    second_in, first_out = after(second_in, first_out)
    second_out = run(second_in, far_gates, 0, None, wide)
    for index in range(1, pairs):
        kind = jnp.bfloat16 if index == last else wide
        first_in, second_out = after(first_in, second_out)
        first_out = run(first_in, near_gates, index, first_out, kind)
        if index == last:
            first_back = swap(first_out)
        second_in, first_out = after(second_in, first_out)
        second_out = run(second_in, far_gates, index, second_out, kind)
        if index == last:
            second_back = swap(second_out)
        normed, second_out = after(normed, second_out)
        own = run(normed, own_gates, index, own, wide)
        first_in, own = after(first_in, own)
    back = jnp.concatenate([first_back, second_back], axis=0)
    final = residual.astype(jnp.float32) + own + back.astype(jnp.float32)
    return final.reshape(tokens.shape).astype(jnp.bfloat16)


def solution(mesh):
    shape = mesh.shape
    group, row, expert = shape["group"], shape["row"], shape["expert"]

    def placed(row_names):
        cells = P("group", row_names + ("expert",), None, None)
        weights = P(row_names, None, None)
        return (cells, P(), P(), P(), P(), P(), cells, cells, weights, weights), cells

    def run(*args):
        experts = row // 2
        tokens, routing = args[0], args[6]
        ranks = row * expert
        dense = routing.shape[-1] == experts and experts % 4 == 0
        dense = dense and tokens.shape[1] == 8 * ranks and (tokens.shape[2] // 2) % ranks == 0
        dense = dense and tokens.shape[0] == group and args[8].shape[1] % (group * expert) == 0
        if dense:
            split = Mesh(
                np.asarray(mesh.devices).reshape(group, row // 4, 2, 2, expert),
                ("group", "pair", "parity", "half", "expert"),
            )
            ins, outs = placed(("pair", "parity", "half"))

            call = jax.shard_map(
                per_device_dense, mesh=split, in_specs=ins, out_specs=outs, check_vma=False
            )
        else:
            ins, outs = placed(("row",))
            call = jax.shard_map(per_device, mesh=mesh, in_specs=ins, out_specs=outs, check_vma=False)
        return call(*args)

    return run
```
